32 devices in a mesh: probe: 4 (over z), gx: 4 (over x, core), gy: 2 (over y).
Axes of the slice: x: 2, y: 2, z: 4, core: 2. Of those that a mesh axis runs over, the one named last changes fastest.
Arguments:
- wave_prev: float32 [4, 128, 256, 256], P('probe', 'gx', 'gy'), may hold values from -6 to 6
- wave_cur: float32 [4, 128, 256, 256], P('probe', 'gx', 'gy'), may hold values from -6 to 6
- courant: float32 [128, 256, 256], P('gx', 'gy'), may hold values from 0.02 to 0.16
- perturb: float32 [4, 128, 256, 256], P('probe', 'gx', 'gy'), may hold values from -4 to 4
- snapshots: bfloat16 [8, 128, 256, 256], P('probe', 'gx', 'gy'), may hold values from -6 to 6
- step_slots: int32 [6], replicated, may hold values from 0 to 7, as said below
- precond: float32 [256], replicated, may hold values from 0.5 to 2
- probe_ids: int32 [4], P('probe'), may hold values from 0 to 255, as said below
Outputs:
- earlier: float32 [4, 128, 256, 256], P('probe', 'gx', 'gy')
- latest: float32 [4, 128, 256, 256], P('probe', 'gx', 'gy')
The draws below stay inside these ranges and needn't reach their ends.
Inputs may be any that keep to these rules, and one draw needn't show every extreme that they name: `step_slots`: distinct slots; 0 and 7 are always among them. `probe_ids`: distinct indices; 0 and 255 are always among them.
All inputs are finite; a program needn't handle non-finite values.
Results may differ from the reference program's by a relative error of at most 0.0003.
Values may be sent and summed in bfloat16 or wider, within the bound.
A program may use at most 192 MiB of HBM per device.

```python
import math
import jax
import jax.numpy as jnp

CZ = 256
STEPS = 4
NPROBE_ALL = 256
PROBES = 4
SLOTS = 8
NSNAP = 6
NX = 128
NY = 256


def pick_distinct(key, count, total):
    inner = jax.random.permutation(key, total - 2)[:count - 2].astype(jnp.int32) + 1
    values = jnp.concatenate([jnp.array([0, total - 1], jnp.int32), inner])
    return jax.random.permutation(jax.random.fold_in(key, 7), values).astype(jnp.int32)


def draw_step_slots(key, part):
    return pick_distinct(jax.random.fold_in(key, 11), NSNAP, SLOTS)


def draw_probe_ids(key, part):
    return pick_distinct(jax.random.fold_in(key, 13), PROBES, NPROBE_ALL)


def steps_of(stream_key, shape, pieces, low, high):
    def one(position, parts):
        draws = jax.random.uniform(jax.random.fold_in(jax.random.fold_in(stream_key, 6), position), (parts,), jnp.float32, low / len(pieces), high / len(pieces))
        return jnp.repeat(jnp.exp(draws), shape[position] // parts).reshape((-1,) + (1,) * (len(shape) - position - 1))

    gain = one(*pieces[0])
    for cut in pieces[1:]:
        gain = gain * one(*cut)
    return gain


def normal_values(rng, extent, spread, limit, cuts=(), kind=jnp.bfloat16):
    result = jax.random.normal(rng, extent, jnp.float32) * spread
    if len(cuts) > 0:
        result = steps_of(rng, extent, cuts, -0.22, 0.18) * result
    return jnp.clip(result, min=-limit, max=limit).astype(kind)


def setup_inputs(seed: int = 0) -> dict:
    key_list = jax.random.split(jax.random.key(seed), 9)
    return {
        "wave_prev": normal_values(key_list[0], (PROBES, NX, NY, CZ), 1.0, 6.0, ((0, 4), (1, 4), (2, 2)), jnp.float32),
        "wave_cur": normal_values(key_list[1], (PROBES, NX, NY, CZ), 1.0, 6.0, ((0, 4), (1, 4), (2, 2)), jnp.float32),
        "courant": jnp.clip(jnp.exp(math.log(0.16) - 2.0794415 * jax.random.uniform(key_list[2], (NX, NY, CZ), jnp.float32) ** steps_of(key_list[2], (NX, NY, CZ), ((0, 4), (1, 2)), -0.2, 0.2)), 0.02, 0.16),
        "perturb": normal_values(key_list[3], (PROBES, NX, NY, CZ), 0.5, 4.0, ((0, 4), (1, 4), (2, 2)), jnp.float32),
        "snapshots": normal_values(key_list[4], (SLOTS, NX, NY, CZ), 1.0, 6.0, ((0, 4), (1, 4), (2, 2))),
        "step_slots": draw_step_slots(jax.random.fold_in(key_list[8], 71), 0),
        "precond": jnp.clip(jnp.exp(jax.random.uniform(key_list[6], (NPROBE_ALL,), jnp.float32, math.log(0.5), math.log(2.0))), 0.5, 2.0),
        "probe_ids": draw_probe_ids(jax.random.fold_in(key_list[8], 71), 0),
    }


COEFFS = (-205.0 / 72.0, 8.0 / 5.0, -1.0 / 5.0, 8.0 / 315.0, -1.0 / 560.0)


def stencil(padded, field):
    extent_x = field.shape[1]
    extent_y = field.shape[2]
    extent_z = field.shape[3]
    total = (3.0 * COEFFS[0]) * field
    for offset in range(1, 5):
        factor = COEFFS[offset]
        along = padded[:, 4 + offset:4 + offset + extent_x, 4:4 + extent_y, 4:4 + extent_z]
        along = along + padded[:, 4 - offset:4 - offset + extent_x, 4:4 + extent_y, 4:4 + extent_z]
        along = along + padded[:, 4:4 + extent_x, 4 + offset:4 + offset + extent_y, 4:4 + extent_z]
        along = along + padded[:, 4:4 + extent_x, 4 - offset:4 - offset + extent_y, 4:4 + extent_z]
        along = along + padded[:, 4:4 + extent_x, 4:4 + extent_y, 4 + offset:4 + offset + extent_z]
        along = along + padded[:, 4:4 + extent_x, 4:4 + extent_y, 4 - offset:4 - offset + extent_z]
        total = total + factor * along
    return total


def reference(wave_prev, wave_cur, courant, perturb, snapshots, step_slots, precond, probe_ids):
    weight = jnp.take(precond, probe_ids.astype(jnp.int32), axis=0)
    scaled = weight[:, None, None, None] * perturb
    frames = jnp.take(snapshots, step_slots.astype(jnp.int32), axis=0).astype(jnp.float32)
    previous = wave_prev
    current = wave_cur
    for index in range(STEPS):
        source = frames[index + 2] - 2.0 * frames[index + 1] + frames[index]
        padded = jnp.pad(current, ((0, 0), (4, 4), (4, 4), (4, 4)))
        laplace = stencil(padded, current)
        following = 2.0 * current - previous + courant[None] * laplace - scaled * source[None]
        previous = current
        current = following
    return previous, current
```

```python
import functools

import jax
import jax.numpy as jnp
import ml_dtypes
import numpy as np
from jax import lax
from jax.experimental import pallas as pl
from jax.experimental.pallas import tpu as pltpu
from jax.sharding import PartitionSpec as P

STEPS = 4
COEFFS = (-205.0 / 72.0, 8.0 / 5.0, -1.0 / 5.0, 8.0 / 315.0, -1.0 / 560.0)
W = 4
PAD = 16
NC = 4
MESH = pl.DeviceIdType.MESH


def band(rows, cols, shift):
    out = np.zeros((rows, cols), np.float64)
    for r in range(rows):
        for k in range(1, 5):
            for c in (r + shift - k, r + shift + k):
                if 0 <= c < cols:
                    out[r, c] += COEFFS[k]
    return out


def halves(matrix):
    high = matrix.astype(ml_dtypes.bfloat16)
    low = (matrix - high.astype(np.float64)).astype(ml_dtypes.bfloat16)
    return high, low


def kernel(
    n_probe,
    n_gx,
    n_gy,
    slots,
    precond,
    ids,
    ymat,
    zmat,
    prev_hbm,
    cur_hbm,
    cou_hbm,
    per_hbm,
    snap_hbm,
    early_hbm,
    late_hbm,
    field,
    cou,
    per,
    own,
    up,
    down,
    frames,
    load_sem,
    out_sem,
    up_send,
    up_recv,
    down_send,
    down_recv,
    halo_send,
    halo_recv,
):
    z = lax.axis_index("probe")
    gx = lax.axis_index("gx")
    gy = lax.axis_index("gy")
    nx, ny = cou.shape[0], cou.shape[1]
    ch = nx // NC
    slot_dev = own.shape[0]
    n_snap = slots.shape[0]
    last_slot = n_probe * slot_dev - 1
    total = (n_snap - 1) * NC
    body_x = pl.ds(W, nx)
    body_y = pl.ds(PAD, ny)

    loads = [
        pltpu.make_async_copy(snap_hbm, own, load_sem.at[0]),
        pltpu.make_async_copy(cur_hbm.at[0], field.at[0, body_x, body_y], load_sem.at[1]),
        pltpu.make_async_copy(prev_hbm.at[0], field.at[1, body_x, body_y], load_sem.at[2]),
        pltpu.make_async_copy(cou_hbm, cou, load_sem.at[3]),
        pltpu.make_async_copy(per_hbm.at[0], per, load_sem.at[4]),
    ]
    for load in loads:
        load.start()

    nz = cou.shape[2]
    zero_plane = jnp.zeros((ny, nz), jnp.float32)
    zero_rows = jnp.zeros((PAD, nz), jnp.float32)
    for b in range(2):
        for x in range(W):
            field[b, x, body_y] = zero_plane
            field[b, W + nx + x, body_y] = zero_plane

        def clear(x, carry, b=b):
            field[b, W + x, pl.ds(0, PAD)] = zero_rows
            field[b, W + x, pl.ds(PAD + ny, PAD)] = zero_rows
            return carry

        lax.fori_loop(0, nx, clear, 0)

    sides = (
        (z < n_probe - 1, {"probe": z + 1}),
        (z > 0, {"probe": z - 1}),
        (gx < n_gx - 1, {"gx": gx + 1}),
        (gx > 0, {"gx": gx - 1}),
        (gy < n_gy - 1, {"gy": gy + 1}),
        (gy > 0, {"gy": gy - 1}),
    )
    barrier = pltpu.get_barrier_semaphore()
    for there, target in sides:

        @pl.when(there)
        def _():
            pl.semaphore_signal(barrier, inc=1, device_id=target, device_id_type=MESH)

    pl.semaphore_wait(barrier, sum(there.astype(jnp.int32) for there, _ in sides))

    halo_out = (
        (pl.ds(nx, W), body_y, pl.ds(0, W), body_y),
        (pl.ds(W, W), body_y, pl.ds(W + nx, W), body_y),
        (body_x, pl.ds(PAD + ny - 8, 8), body_x, pl.ds(PAD - 8, 8)),
        (body_x, pl.ds(PAD, 8), body_x, pl.ds(PAD + ny, 8)),
    )
    back = (1, 0, 3, 2)

    def halo(e, side):
        sx, sy, dx, dy = halo_out[side]
        return pltpu.make_async_remote_copy(
            src_ref=field.at[e % 2, sx, sy],
            dst_ref=field.at[e % 2, dx, dy],
            send_sem=halo_send.at[e, side],
            recv_sem=halo_recv.at[e, side],
            device_id=sides[2 + side][1],
            device_id_type=MESH,
        )

    def halo_start(e):
        for side in range(4):

            @pl.when(sides[2 + side][0])
            def _():
                halo(e, side).start()

    def halo_wait(e):
        for side in range(4):

            @pl.when(sides[2 + side][0])
            def _():
                halo(e, side).wait_send()
                halo(e, back[side]).wait_recv()

    at = [slots[j] for j in range(n_snap)]
    owner = [lax.div(a, slot_dev) for a in at]
    first_pos = jnp.int32(0)
    last_pos = jnp.int32(0)
    for j in range(n_snap):
        first_pos = jnp.where(at[j] == 0, j, first_pos)
        last_pos = jnp.where(at[j] == last_slot, j, last_pos)

    def relay(k, buf, skipped, at_source, forwards, target, send, recv):
        def link(i):
            return pltpu.make_async_remote_copy(
                src_ref=buf.at[i],
                dst_ref=buf.at[i],
                send_sem=send.at[i],
                recv_sem=recv.at[i],
                device_id=target,
                device_id_type=MESH,
            )

        @pl.when((k >= 0) & (k < total))
        def _():
            m = lax.div(k, NC)
            c = k - m * NC
            position = m + jnp.where(m >= skipped, 1, 0)
            slot = slots[position]
            mine = lax.div(slot, slot_dev) == z
            which = lax.rem(slot, slot_dev)

            @pl.when(at_source)
            def _():
                def fill(i, carry):
                    buf[k, i] = own[which, c * ch + i]
                    return carry

                lax.fori_loop(0, ch, fill, 0)

            @pl.when(jnp.logical_not(at_source))
            def _():
                link(k).wait_recv()

                def fill(i, carry):
                    buf[k, i] = lax.select(mine, own[which, c * ch + i], buf[k, i])
                    return carry

                lax.fori_loop(0, ch, fill, 0)

            @pl.when(forwards)
            def _():
                link(k).start()

        return link

    def comm(s):
        relay(s - z, up, last_pos, z == 0, z < n_probe - 1, {"probe": z + 1}, up_send, up_recv)
        relay(
            s - (n_probe - 1 - z),
            down,
            first_pos,
            z == n_probe - 1,
            z > 0,
            {"probe": z - 1},
            down_send,
            down_recv,
        )

    def snapshot(j, c, i):
        def pick(buf, skipped):
            if j == 0:
                return buf[c, i]
            before = buf[(j - 1) * NC + c, i]
            if j == n_snap - 1:
                return before
            return lax.select(skipped < j, before, buf[j * NC + c, i])

        from_up = (owner[j] <= z) & (last_pos != j)
        return lax.select(from_up, pick(up, last_pos), pick(down, first_pos))

    weight = precond[ids[0]]

    def plane(n, c, i):
        a, b = n % 2, 1 - n % 2
        x = c * ch + i
        if n == 0:
            frames[0, x] = snapshot(0, c, i)
            frames[1, x] = snapshot(1, c, i)
        newest = snapshot(n + 2, c, i)
        if n < STEPS - 1:
            frames[(n + 2) % 3, x] = newest
        source = (
            newest.astype(jnp.float32)
            - 2.0 * frames[(n + 1) % 3, x].astype(jnp.float32)
            + frames[n % 3, x].astype(jnp.float32)
        )
        padded = field[a, x + W]
        high = padded.astype(jnp.bfloat16)
        low = (padded - high.astype(jnp.float32)).astype(jnp.bfloat16)
        lap = jnp.dot(
            ymat[...],
            jnp.concatenate([high, low, high], axis=0),
            preferred_element_type=jnp.float32,
        )
        high = high[PAD : PAD + ny]
        low = low[PAD : PAD + ny]
        lap = lap + jnp.dot(
            jnp.concatenate([high, low, high], axis=1),
            zmat[...],
            preferred_element_type=jnp.float32,
        )
        here = field[a, x + W, body_y]
        lap = lap + (3.0 * COEFFS[0]) * here
        for k in range(1, 5):
            lap = lap + COEFFS[k] * (field[a, x + W + k, body_y] + field[a, x + W - k, body_y])
        field[b, x + W, body_y] = (
            2.0 * here - field[b, x + W, body_y] + cou[x] * lap - (weight * per[x]) * source
        )

    for load in loads[:2]:
        load.wait()
    halo_start(0)

    def lead(s, carry):
        comm(s)
        return carry

    start = 2 * NC + n_probe - 1
    lax.fori_loop(0, start, lead, 0)
    for load in loads[2:]:
        load.wait()

    early = pltpu.make_async_copy(field.at[1, body_x, body_y], early_hbm.at[0], out_sem.at[NC])

    def late(c):
        return pltpu.make_async_copy(
            field.at[0, pl.ds(W + c * ch, ch), body_y],
            late_hbm.at[0, pl.ds(c * ch, ch)],
            out_sem.at[c],
        )

    for n in range(STEPS):
        def chunk(c, carry, n=n):
            if n < STEPS - 1:
                comm(start + NC * n + c)

            def planes(i, carry):
                plane(n, c, i)
                return carry

            lax.fori_loop(0, ch, planes, 0)
            if n == STEPS - 1:
                late(c).start()
            return carry

        halo_wait(n)
        if n == STEPS - 1:
            early.start()
        lax.fori_loop(0, NC, chunk, 0)
        if n < STEPS - 1:
            halo_start(n + 1)

    def finish(k, carry):
        @pl.when(z < n_probe - 1)
        def _():
            relay_link(up, up_send, up_recv, {"probe": z + 1}, k).wait_send()

        @pl.when(z > 0)
        def _():
            relay_link(down, down_send, down_recv, {"probe": z - 1}, k).wait_send()

        return carry

    lax.fori_loop(0, total, finish, 0)
    early.wait()

    def flush(c, carry):
        late(c).wait()
        return carry

    lax.fori_loop(0, NC, flush, 0)


def relay_link(buf, send, recv, target, i):
    return pltpu.make_async_remote_copy(
        src_ref=buf.at[i],
        dst_ref=buf.at[i],
        send_sem=send.at[i],
        recv_sem=recv.at[i],
        device_id=target,
        device_id_type=MESH,
    )


def shards(sizes, wave_prev, wave_cur, courant, perturb, snapshots, step_slots, precond, probe_ids):
    nx, ny, nz = courant.shape
    slot_dev = snapshots.shape[0]
    total = (step_slots.shape[0] - 1) * NC
    y_high, y_low = halves(band(ny, ny + 2 * PAD, PAD))
    z_high, z_low = halves(band(nz, nz, 0))
    ymat = jnp.asarray(np.concatenate([y_high, y_high, y_low], axis=1))
    zmat = jnp.asarray(np.concatenate([z_high, z_high, z_low], axis=0))
    smem = pl.BlockSpec(memory_space=pltpu.SMEM)
    vmem = pl.BlockSpec(memory_space=pltpu.VMEM)
    hbm = pl.BlockSpec(memory_space=pl.ANY)
    wave = jax.ShapeDtypeStruct(wave_cur.shape, jnp.float32)
    dma = pltpu.SemaphoreType.DMA
    messages = pltpu.VMEM((total, nx // NC, ny, nz), jnp.bfloat16)
    return pl.pallas_call(
        functools.partial(kernel, *sizes),
        out_shape=(wave, wave),
        in_specs=[smem, smem, smem, vmem, vmem] + [hbm] * 5,
        out_specs=(hbm, hbm),
        scratch_shapes=[
            pltpu.VMEM((2, nx + 2 * W, ny + 2 * PAD, nz), jnp.float32),
            pltpu.VMEM((nx, ny, nz), jnp.float32),
            pltpu.VMEM((nx, ny, nz), jnp.float32),
            pltpu.VMEM((slot_dev, nx, ny, nz), jnp.bfloat16),
            messages,
            messages,
            pltpu.VMEM((3, nx, ny, nz), jnp.bfloat16),
            dma((5,)),
            dma((NC + 1,)),
            dma((total,)),
            dma((total,)),
            dma((total,)),
            dma((total,)),
            dma((STEPS, 4)),
            dma((STEPS, 4)),
        ],
        compiler_params=pltpu.CompilerParams(
            collective_id=0, has_side_effects=True, vmem_limit_bytes=60 * 1024 * 1024
        ),
    )(
        step_slots,
        precond,
        probe_ids,
        ymat,
        zmat,
        wave_prev,
        wave_cur,
        courant,
        perturb,
        snapshots,
    )


def solution(mesh):
    placed = (
        P("probe", "gx", "gy", None),
        P("probe", "gx", "gy", None),
        P("gx", "gy", None),
        P("probe", "gx", "gy", None),
        P("probe", "gx", "gy", None),
        P(),
        P(),
        P("probe"),
    )
    sizes = (mesh.shape["probe"], mesh.shape["gx"], mesh.shape["gy"])
    return jax.shard_map(
        functools.partial(shards, sizes),
        mesh=mesh,
        in_specs=placed,
        out_specs=(P("probe", "gx", "gy", None), P("probe", "gx", "gy", None)),
        check_vma=False,
    )
```

```python
import functools

import jax
import jax.numpy as jnp
import ml_dtypes
import numpy as np
from jax import lax
from jax.experimental import pallas as pl
from jax.experimental.pallas import tpu as pltpu
from jax.sharding import PartitionSpec as P

STEPS = 4
COEFFS = (-205.0 / 72.0, 8.0 / 5.0, -1.0 / 5.0, 8.0 / 315.0, -1.0 / 560.0)
W = 4
PAD = 16
NC = 8
LAG = 2
MESH = pl.DeviceIdType.MESH


def band(rows, cols, shift):
    out = np.zeros((rows, cols), np.float64)
    for r in range(rows):
        for k in range(1, 5):
            for c in (r + shift - k, r + shift + k):
                if 0 <= c < cols:
                    out[r, c] += COEFFS[k]
    return out


def halves(matrix):
    high = matrix.astype(ml_dtypes.bfloat16)
    low = (matrix - high.astype(np.float64)).astype(ml_dtypes.bfloat16)
    return high, low


def kernel(
    n_probe,
    n_gx,
    n_gy,
    slots,
    precond,
    ids,
    ymat,
    zmat,
    prev_hbm,
    cur_hbm,
    cou_hbm,
    per_hbm,
    snap_hbm,
    early_hbm,
    late_hbm,
    field,
    cou,
    per,
    own,
    up,
    down,
    frames,
    load_sem,
    out_sem,
    up_send,
    up_recv,
    down_send,
    down_recv,
    halo_send,
    halo_recv,
):
    z = lax.axis_index("probe")
    gx = lax.axis_index("gx")
    gy = lax.axis_index("gy")
    nx, ny = cou.shape[0], cou.shape[1]
    ch = nx // NC
    slot_dev = own.shape[0]
    n_snap = slots.shape[0]
    last_slot = n_probe * slot_dev - 1
    total = (n_snap - 1) * NC
    body_x = pl.ds(W, nx)
    body_y = pl.ds(PAD, ny)

    loads = [
        pltpu.make_async_copy(snap_hbm, own, load_sem.at[0]),
        pltpu.make_async_copy(cur_hbm.at[0], field.at[0, body_x, body_y], load_sem.at[1]),
        pltpu.make_async_copy(prev_hbm.at[0], field.at[1, body_x, body_y], load_sem.at[2]),
        pltpu.make_async_copy(cou_hbm, cou, load_sem.at[3]),
        pltpu.make_async_copy(per_hbm.at[0], per, load_sem.at[4]),
    ]
    for load in loads:
        load.start()

    nz = cou.shape[2]
    zero_plane = jnp.zeros((ny, nz), jnp.float32)
    zero_rows = jnp.zeros((PAD, nz), jnp.float32)
    for b in range(2):
        for x in range(W):
            field[b, x, body_y] = zero_plane
            field[b, W + nx + x, body_y] = zero_plane

        def clear(x, carry, b=b):
            field[b, W + x, pl.ds(0, PAD)] = zero_rows
            field[b, W + x, pl.ds(PAD + ny, PAD)] = zero_rows
            return carry

        lax.fori_loop(0, nx, clear, 0)

    sides = (
        (z < n_probe - 1, {"probe": z + 1}),
        (z > 0, {"probe": z - 1}),
        (gx < n_gx - 1, {"gx": gx + 1}),
        (gx > 0, {"gx": gx - 1}),
        (gy < n_gy - 1, {"gy": gy + 1}),
        (gy > 0, {"gy": gy - 1}),
    )
    barrier = pltpu.get_barrier_semaphore()
    for there, target in sides:

        @pl.when(there)
        def _():
            pl.semaphore_signal(barrier, inc=1, device_id=target, device_id_type=MESH)

    pl.semaphore_wait(barrier, sum(there.astype(jnp.int32) for there, _ in sides))

    halo_out = (
        (pl.ds(nx, W), body_y, pl.ds(0, W), body_y),
        (pl.ds(W, W), body_y, pl.ds(W + nx, W), body_y),
        (body_x, pl.ds(PAD + ny - 8, 8), body_x, pl.ds(PAD - 8, 8)),
        (body_x, pl.ds(PAD, 8), body_x, pl.ds(PAD + ny, 8)),
    )
    back = (1, 0, 3, 2)

    def halo(e, side):
        sx, sy, dx, dy = halo_out[side]
        return pltpu.make_async_remote_copy(
            src_ref=field.at[e % 2, sx, sy],
            dst_ref=field.at[e % 2, dx, dy],
            send_sem=halo_send.at[e, side],
            recv_sem=halo_recv.at[e, side],
            device_id=sides[2 + side][1],
            device_id_type=MESH,
        )

    def halo_start(e):
        for side in range(4):

            @pl.when(sides[2 + side][0])
            def _():
                halo(e, side).start()

    def halo_wait(e):
        for side in range(4):

            @pl.when(sides[2 + side][0])
            def _():
                halo(e, side).wait_send()
                halo(e, back[side]).wait_recv()

    at = [slots[j] for j in range(n_snap)]
    owner = [lax.div(a, slot_dev) for a in at]
    first_pos = jnp.int32(0)
    last_pos = jnp.int32(0)
    for j in range(n_snap):
        first_pos = jnp.where(at[j] == 0, j, first_pos)
        last_pos = jnp.where(at[j] == last_slot, j, last_pos)

    def relay(k, buf, skipped, at_source, forwards, target, send, recv):
        def link(i):
            return pltpu.make_async_remote_copy(
                src_ref=buf.at[i],
                dst_ref=buf.at[i],
                send_sem=send.at[i],
                recv_sem=recv.at[i],
                device_id=target,
                device_id_type=MESH,
            )

        @pl.when((k >= 0) & (k < total))
        def _():
            m = lax.div(k, NC)
            c = k - m * NC
            position = m + jnp.where(m >= skipped, 1, 0)
            slot = slots[position]
            mine = lax.div(slot, slot_dev) == z
            which = lax.rem(slot, slot_dev)

            @pl.when(at_source)
            def _():
                def fill(i, carry):
                    buf[k, i] = own[which, c * ch + i]
                    return carry

                lax.fori_loop(0, ch, fill, 0)

            @pl.when(jnp.logical_not(at_source))
            def _():
                link(k).wait_recv()

                def fill(i, carry):
                    buf[k, i] = lax.select(mine, own[which, c * ch + i], buf[k, i])
                    return carry

                lax.fori_loop(0, ch, fill, 0)

            @pl.when(forwards)
            def _():
                link(k).start()

        return link

    def comm(s):
        relay(s - LAG * z, up, last_pos, z == 0, z < n_probe - 1, {"probe": z + 1}, up_send, up_recv)
        relay(
            s - LAG * (n_probe - 1 - z),
            down,
            first_pos,
            z == n_probe - 1,
            z > 0,
            {"probe": z - 1},
            down_send,
            down_recv,
        )

    def snapshot(j, c, i):
        def pick(buf, skipped):
            if j == 0:
                return buf[c, i]
            before = buf[(j - 1) * NC + c, i]
            if j == n_snap - 1:
                return before
            return lax.select(skipped < j, before, buf[j * NC + c, i])

        from_up = (owner[j] <= z) & (last_pos != j)
        return lax.select(from_up, pick(up, last_pos), pick(down, first_pos))

    weight = precond[ids[0]]

    def plane(n, c, i):
        a, b = n % 2, 1 - n % 2
        x = c * ch + i
        if n == 0:
            frames[0, x] = snapshot(0, c, i)
            frames[1, x] = snapshot(1, c, i)
        newest = snapshot(n + 2, c, i)
        if n < STEPS - 1:
            frames[(n + 2) % 3, x] = newest
        source = (
            newest.astype(jnp.float32)
            - 2.0 * frames[(n + 1) % 3, x].astype(jnp.float32)
            + frames[n % 3, x].astype(jnp.float32)
        )
        padded = field[a, x + W]
        high = padded.astype(jnp.bfloat16)
        low = (padded - high.astype(jnp.float32)).astype(jnp.bfloat16)
        lap = jnp.dot(
            ymat[...],
            jnp.concatenate([high, low, high], axis=0),
            preferred_element_type=jnp.float32,
        )
        high = high[PAD : PAD + ny]
        low = low[PAD : PAD + ny]
        lap = lap + jnp.dot(
            jnp.concatenate([high, low, high], axis=1),
            zmat[...],
            preferred_element_type=jnp.float32,
        )
        here = field[a, x + W, body_y]
        lap = lap + (3.0 * COEFFS[0]) * here
        for k in range(1, 5):
            lap = lap + COEFFS[k] * (field[a, x + W + k, body_y] + field[a, x + W - k, body_y])
        field[b, x + W, body_y] = (
            2.0 * here - field[b, x + W, body_y] + cou[x] * lap - (weight * per[x]) * source
        )

    for load in loads[:2]:
        load.wait()
    halo_start(0)

    def lead(s, carry):
        comm(s)
        return carry

    start = 2 * NC + LAG * (n_probe - 1)
    lax.fori_loop(0, start, lead, 0)
    for load in loads[2:]:
        load.wait()

    early = pltpu.make_async_copy(field.at[1, body_x, body_y], early_hbm.at[0], out_sem.at[NC])

    def late(c):
        return pltpu.make_async_copy(
            field.at[0, pl.ds(W + c * ch, ch), body_y],
            late_hbm.at[0, pl.ds(c * ch, ch)],
            out_sem.at[c],
        )

    for n in range(STEPS):
        def chunk(c, carry, n=n):
            if n < STEPS - 1:
                comm(start + NC * n + c)

            def planes(i, carry):
                plane(n, c, i)
                return carry

            lax.fori_loop(0, ch, planes, 0)
            if n == STEPS - 1:
                late(c).start()
            return carry

        halo_wait(n)
        if n == STEPS - 1:
            early.start()
        lax.fori_loop(0, NC, chunk, 0)
        if n < STEPS - 1:
            halo_start(n + 1)

    def finish(k, carry):
        @pl.when(z < n_probe - 1)
        def _():
            relay_link(up, up_send, up_recv, {"probe": z + 1}, k).wait_send()

        @pl.when(z > 0)
        def _():
            relay_link(down, down_send, down_recv, {"probe": z - 1}, k).wait_send()

        return carry

    lax.fori_loop(0, total, finish, 0)
    early.wait()

    def flush(c, carry):
        late(c).wait()
        return carry

    lax.fori_loop(0, NC, flush, 0)


def relay_link(buf, send, recv, target, i):
    return pltpu.make_async_remote_copy(
        src_ref=buf.at[i],
        dst_ref=buf.at[i],
        send_sem=send.at[i],
        recv_sem=recv.at[i],
        device_id=target,
        device_id_type=MESH,
    )


def shards(sizes, wave_prev, wave_cur, courant, perturb, snapshots, step_slots, precond, probe_ids):
    nx, ny, nz = courant.shape
    slot_dev = snapshots.shape[0]
    total = (step_slots.shape[0] - 1) * NC
    y_high, y_low = halves(band(ny, ny + 2 * PAD, PAD))
    z_high, z_low = halves(band(nz, nz, 0))
    ymat = jnp.asarray(np.concatenate([y_high, y_high, y_low], axis=1))
    zmat = jnp.asarray(np.concatenate([z_high, z_high, z_low], axis=0))
    smem = pl.BlockSpec(memory_space=pltpu.SMEM)
    vmem = pl.BlockSpec(memory_space=pltpu.VMEM)
    hbm = pl.BlockSpec(memory_space=pl.ANY)
    wave = jax.ShapeDtypeStruct(wave_cur.shape, jnp.float32)
    dma = pltpu.SemaphoreType.DMA
    messages = pltpu.VMEM((total, nx // NC, ny, nz), jnp.bfloat16)
    return pl.pallas_call(
        functools.partial(kernel, *sizes),
        out_shape=(wave, wave),
        in_specs=[smem, smem, smem, vmem, vmem] + [hbm] * 5,
        out_specs=(hbm, hbm),
        scratch_shapes=[
            pltpu.VMEM((2, nx + 2 * W, ny + 2 * PAD, nz), jnp.float32),
            pltpu.VMEM((nx, ny, nz), jnp.float32),
            pltpu.VMEM((nx, ny, nz), jnp.float32),
            pltpu.VMEM((slot_dev, nx, ny, nz), jnp.bfloat16),
            messages,
            messages,
            pltpu.VMEM((3, nx, ny, nz), jnp.bfloat16),
            dma((5,)),
            dma((NC + 1,)),
            dma((total,)),
            dma((total,)),
            dma((total,)),
            dma((total,)),
            dma((STEPS, 4)),
            dma((STEPS, 4)),
        ],
        compiler_params=pltpu.CompilerParams(
            collective_id=0, has_side_effects=True, vmem_limit_bytes=60 * 1024 * 1024
        ),
    )(
        step_slots,
        precond,
        probe_ids,
        ymat,
        zmat,
        wave_prev,
        wave_cur,
        courant,
        perturb,
        snapshots,
    )


def solution(mesh):
    placed = (
        P("probe", "gx", "gy", None),
        P("probe", "gx", "gy", None),
        P("gx", "gy", None),
        P("probe", "gx", "gy", None),
        P("probe", "gx", "gy", None),
        P(),
        P(),
        P("probe"),
    )
    sizes = (mesh.shape["probe"], mesh.shape["gx"], mesh.shape["gy"])
    return jax.shard_map(
        functools.partial(shards, sizes),
        mesh=mesh,
        in_specs=placed,
        out_specs=(P("probe", "gx", "gy", None), P("probe", "gx", "gy", None)),
        check_vma=False,
    )
```

```python
import functools

import jax
import jax.numpy as jnp
import ml_dtypes
import numpy as np
from jax import lax
from jax.experimental import pallas as pl
from jax.experimental.pallas import tpu as pltpu
from jax.sharding import PartitionSpec as P

STEPS = 4
COEFFS = (-205.0 / 72.0, 8.0 / 5.0, -1.0 / 5.0, 8.0 / 315.0, -1.0 / 560.0)
W = 4
PAD = 16
NC = 16
LAG = 3
MESH = pl.DeviceIdType.MESH


def band(rows, cols, shift):
    out = np.zeros((rows, cols), np.float64)
    for r in range(rows):
        for k in range(1, 5):
            for c in (r + shift - k, r + shift + k):
                if 0 <= c < cols:
                    out[r, c] += COEFFS[k]
    return out


def halves(matrix):
    high = matrix.astype(ml_dtypes.bfloat16)
    low = (matrix - high.astype(np.float64)).astype(ml_dtypes.bfloat16)
    return high, low


def kernel(
    n_probe,
    n_gx,
    n_gy,
    slots,
    precond,
    ids,
    ymat,
    zmat,
    prev_hbm,
    cur_hbm,
    cou_hbm,
    per_hbm,
    snap_hbm,
    early_hbm,
    late_hbm,
    field,
    cou,
    per,
    own,
    up,
    down,
    frames,
    load_sem,
    out_sem,
    up_send,
    up_recv,
    down_send,
    down_recv,
    halo_send,
    halo_recv,
):
    z = lax.axis_index("probe")
    gx = lax.axis_index("gx")
    gy = lax.axis_index("gy")
    nx, ny = cou.shape[0], cou.shape[1]
    ch = nx // NC
    slot_dev = own.shape[0]
    n_snap = slots.shape[0]
    last_slot = n_probe * slot_dev - 1
    total = (n_snap - 1) * NC
    body_x = pl.ds(W, nx)
    body_y = pl.ds(PAD, ny)

    loads = [
        pltpu.make_async_copy(snap_hbm, own, load_sem.at[0]),
        pltpu.make_async_copy(cur_hbm.at[0], field.at[0, body_x, body_y], load_sem.at[1]),
        pltpu.make_async_copy(prev_hbm.at[0], field.at[1, body_x, body_y], load_sem.at[2]),
        pltpu.make_async_copy(cou_hbm, cou, load_sem.at[3]),
        pltpu.make_async_copy(per_hbm.at[0], per, load_sem.at[4]),
    ]
    for load in loads:
        load.start()

    nz = cou.shape[2]
    zero_plane = jnp.zeros((ny, nz), jnp.float32)
    zero_rows = jnp.zeros((PAD, nz), jnp.float32)
    for b in range(2):
        for x in range(W):
            field[b, x, body_y] = zero_plane
            field[b, W + nx + x, body_y] = zero_plane

        def clear(x, carry, b=b):
            field[b, W + x, pl.ds(0, PAD)] = zero_rows
            field[b, W + x, pl.ds(PAD + ny, PAD)] = zero_rows
            return carry

        lax.fori_loop(0, nx, clear, 0)

    sides = (
        (z < n_probe - 1, {"probe": z + 1}),
        (z > 0, {"probe": z - 1}),
        (gx < n_gx - 1, {"gx": gx + 1}),
        (gx > 0, {"gx": gx - 1}),
        (gy < n_gy - 1, {"gy": gy + 1}),
        (gy > 0, {"gy": gy - 1}),
    )
    barrier = pltpu.get_barrier_semaphore()
    for there, target in sides:

        @pl.when(there)
        def _():
            pl.semaphore_signal(barrier, inc=1, device_id=target, device_id_type=MESH)

    pl.semaphore_wait(barrier, sum(there.astype(jnp.int32) for there, _ in sides))

    halo_out = (
        (pl.ds(nx, W), body_y, pl.ds(0, W), body_y),
        (pl.ds(W, W), body_y, pl.ds(W + nx, W), body_y),
        (body_x, pl.ds(PAD + ny - 8, 8), body_x, pl.ds(PAD - 8, 8)),
        (body_x, pl.ds(PAD, 8), body_x, pl.ds(PAD + ny, 8)),
    )
    back = (1, 0, 3, 2)

    def halo(e, side):
        sx, sy, dx, dy = halo_out[side]
        return pltpu.make_async_remote_copy(
            src_ref=field.at[e % 2, sx, sy],
            dst_ref=field.at[e % 2, dx, dy],
            send_sem=halo_send.at[e, side],
            recv_sem=halo_recv.at[e, side],
            device_id=sides[2 + side][1],
            device_id_type=MESH,
        )

    def halo_start(e):
        for side in range(4):

            @pl.when(sides[2 + side][0])
            def _():
                halo(e, side).start()

    def halo_wait(e):
        for side in range(4):

            @pl.when(sides[2 + side][0])
            def _():
                halo(e, side).wait_send()
                halo(e, back[side]).wait_recv()

    at = [slots[j] for j in range(n_snap)]
    owner = [lax.div(a, slot_dev) for a in at]
    first_pos = jnp.int32(0)
    last_pos = jnp.int32(0)
    for j in range(n_snap):
        first_pos = jnp.where(at[j] == 0, j, first_pos)
        last_pos = jnp.where(at[j] == last_slot, j, last_pos)

    def relay(k, buf, skipped, at_source, forwards, target, send, recv):
        def link(i):
            return pltpu.make_async_remote_copy(
                src_ref=buf.at[i],
                dst_ref=buf.at[i],
                send_sem=send.at[i],
                recv_sem=recv.at[i],
                device_id=target,
                device_id_type=MESH,
            )

        @pl.when((k >= 0) & (k < total))
        def _():
            m = lax.div(k, NC)
            c = k - m * NC
            position = m + jnp.where(m >= skipped, 1, 0)
            slot = slots[position]
            mine = lax.div(slot, slot_dev) == z
            which = lax.rem(slot, slot_dev)

            @pl.when(at_source)
            def _():
                def fill(i, carry):
                    buf[k, i] = own[which, c * ch + i]
                    return carry

                lax.fori_loop(0, ch, fill, 0)

            @pl.when(jnp.logical_not(at_source))
            def _():
                link(k).wait_recv()

                def fill(i, carry):
                    buf[k, i] = lax.select(mine, own[which, c * ch + i], buf[k, i])
                    return carry

                lax.fori_loop(0, ch, fill, 0)

            @pl.when(forwards)
            def _():
                link(k).start()

        return link

    def comm(s):
        relay(s - LAG * z, up, last_pos, z == 0, z < n_probe - 1, {"probe": z + 1}, up_send, up_recv)
        relay(
            s - LAG * (n_probe - 1 - z),
            down,
            first_pos,
            z == n_probe - 1,
            z > 0,
            {"probe": z - 1},
            down_send,
            down_recv,
        )

    def snapshot(j, c, i):
        def pick(buf, skipped):
            if j == 0:
                return buf[c, i]
            before = buf[(j - 1) * NC + c, i]
            if j == n_snap - 1:
                return before
            return lax.select(skipped < j, before, buf[j * NC + c, i])

        from_up = (owner[j] <= z) & (last_pos != j)
        return lax.select(from_up, pick(up, last_pos), pick(down, first_pos))

    weight = precond[ids[0]]

    def plane(n, c, i):
        a, b = n % 2, 1 - n % 2
        x = c * ch + i
        if n == 0:
            frames[0, x] = snapshot(0, c, i)
            frames[1, x] = snapshot(1, c, i)
        newest = snapshot(n + 2, c, i)
        if n < STEPS - 1:
            frames[(n + 2) % 3, x] = newest
        source = (
            newest.astype(jnp.float32)
            - 2.0 * frames[(n + 1) % 3, x].astype(jnp.float32)
            + frames[n % 3, x].astype(jnp.float32)
        )
        padded = field[a, x + W]
        high = padded.astype(jnp.bfloat16)
        low = (padded - high.astype(jnp.float32)).astype(jnp.bfloat16)
        lap = jnp.dot(
            ymat[...],
            jnp.concatenate([high, low, high], axis=0),
            preferred_element_type=jnp.float32,
        )
        high = high[PAD : PAD + ny]
        low = low[PAD : PAD + ny]
        lap = lap + jnp.dot(
            jnp.concatenate([high, low, high], axis=1),
            zmat[...],
            preferred_element_type=jnp.float32,
        )
        here = field[a, x + W, body_y]
        lap = lap + (3.0 * COEFFS[0]) * here
        for k in range(1, 5):
            lap = lap + COEFFS[k] * (field[a, x + W + k, body_y] + field[a, x + W - k, body_y])
        field[b, x + W, body_y] = (
            2.0 * here - field[b, x + W, body_y] + cou[x] * lap - (weight * per[x]) * source
        )

    for load in loads[:2]:
        load.wait()
    halo_start(0)

    def lead(s, carry):
        comm(s)
        return carry

    start = 2 * NC + LAG * (n_probe - 1)
    lax.fori_loop(0, start, lead, 0)
    for load in loads[2:]:
        load.wait()

    early = pltpu.make_async_copy(field.at[1, body_x, body_y], early_hbm.at[0], out_sem.at[NC])

    def late(c):
        return pltpu.make_async_copy(
            field.at[0, pl.ds(W + c * ch, ch), body_y],
            late_hbm.at[0, pl.ds(c * ch, ch)],
            out_sem.at[c],
        )

    for n in range(STEPS):
        def chunk(c, carry, n=n):
            if n < STEPS - 1:
                comm(start + NC * n + c)

            def planes(i, carry):
                plane(n, c, i)
                return carry

            lax.fori_loop(0, ch, planes, 0)
            if n == STEPS - 1:
                late(c).start()
            return carry

        halo_wait(n)
        if n == STEPS - 1:
            early.start()
        lax.fori_loop(0, NC, chunk, 0)
        if n < STEPS - 1:
            halo_start(n + 1)

    def finish(k, carry):
        @pl.when(z < n_probe - 1)
        def _():
            relay_link(up, up_send, up_recv, {"probe": z + 1}, k).wait_send()

        @pl.when(z > 0)
        def _():
            relay_link(down, down_send, down_recv, {"probe": z - 1}, k).wait_send()

        return carry

    lax.fori_loop(0, total, finish, 0)
    early.wait()

    def flush(c, carry):
        late(c).wait()
        return carry

    lax.fori_loop(0, NC, flush, 0)


def relay_link(buf, send, recv, target, i):
    return pltpu.make_async_remote_copy(
        src_ref=buf.at[i],
        dst_ref=buf.at[i],
        send_sem=send.at[i],
        recv_sem=recv.at[i],
        device_id=target,
        device_id_type=MESH,
    )


def shards(sizes, wave_prev, wave_cur, courant, perturb, snapshots, step_slots, precond, probe_ids):
    nx, ny, nz = courant.shape
    slot_dev = snapshots.shape[0]
    total = (step_slots.shape[0] - 1) * NC
    y_high, y_low = halves(band(ny, ny + 2 * PAD, PAD))
    z_high, z_low = halves(band(nz, nz, 0))
    ymat = jnp.asarray(np.concatenate([y_high, y_high, y_low], axis=1))
    zmat = jnp.asarray(np.concatenate([z_high, z_high, z_low], axis=0))
    smem = pl.BlockSpec(memory_space=pltpu.SMEM)
    vmem = pl.BlockSpec(memory_space=pltpu.VMEM)
    hbm = pl.BlockSpec(memory_space=pl.ANY)
    wave = jax.ShapeDtypeStruct(wave_cur.shape, jnp.float32)
    dma = pltpu.SemaphoreType.DMA
    messages = pltpu.VMEM((total, nx // NC, ny, nz), jnp.bfloat16)
    return pl.pallas_call(
        functools.partial(kernel, *sizes),
        out_shape=(wave, wave),
        in_specs=[smem, smem, smem, vmem, vmem] + [hbm] * 5,
        out_specs=(hbm, hbm),
        scratch_shapes=[
            pltpu.VMEM((2, nx + 2 * W, ny + 2 * PAD, nz), jnp.float32),
            pltpu.VMEM((nx, ny, nz), jnp.float32),
            pltpu.VMEM((nx, ny, nz), jnp.float32),
            pltpu.VMEM((slot_dev, nx, ny, nz), jnp.bfloat16),
            messages,
            messages,
            pltpu.VMEM((3, nx, ny, nz), jnp.bfloat16),
            dma((5,)),
            dma((NC + 1,)),
            dma((total,)),
            dma((total,)),
            dma((total,)),
            dma((total,)),
            dma((STEPS, 4)),
            dma((STEPS, 4)),
        ],
        compiler_params=pltpu.CompilerParams(
            collective_id=0, has_side_effects=True, vmem_limit_bytes=60 * 1024 * 1024
        ),
    )(
        step_slots,
        precond,
        probe_ids,
        ymat,
        zmat,
        wave_prev,
        wave_cur,
        courant,
        perturb,
        snapshots,
    )


def solution(mesh):
    placed = (
        P("probe", "gx", "gy", None),
        P("probe", "gx", "gy", None),
        P("gx", "gy", None),
        P("probe", "gx", "gy", None),
        P("probe", "gx", "gy", None),
        P(),
        P(),
        P("probe"),
    )
    sizes = (mesh.shape["probe"], mesh.shape["gx"], mesh.shape["gy"])
    return jax.shard_map(
        functools.partial(shards, sizes),
        mesh=mesh,
        in_specs=placed,
        out_specs=(P("probe", "gx", "gy", None), P("probe", "gx", "gy", None)),
        check_vma=False,
    )
```
